256 devices in a mesh: gx: 32 (over z, x_lo, core), gy: 8 (over y, x_hi).
Axes of the slice: x: 4 (x_hi: 2, x_lo: 2; x = x_hi * 2 + x_lo), y: 4, z: 8, core: 2. Of those that a mesh axis runs over, the one named last changes fastest.
Arguments:
- vectors: bfloat16 [128, 64, 128, 128], P('gx', 'gy'), may hold values from -6 to 6
- hamiltonian: bfloat16 [128, 64, 9, 128, 128], P('gx', 'gy'), may hold values from -0.125 to 0.125
- neighbours: int32 [128, 64, 9], P('gx', 'gy'), may hold values from 0 to 8, each once within a row
Outputs:
- filtered: float32 [128, 64, 128, 128], P('gx', 'gy')
The draws below stay inside these ranges and needn't reach their ends.
Inputs may be any that keep to these rules, and one draw needn't show every extreme that they name: `neighbours`: each cell's list names every offset code 0 to 8 exactly once, in any order.
All inputs are finite; a program needn't handle non-finite values.
Results may differ from the reference program's by a relative error of at most 0.0034.
Values may be sent and summed in bfloat16 or wider, within the bound.
No kernel may reach another device: no remote copies, remote signals or barrier semaphores. Data moves between devices by JAX's collectives and lax.ppermute only.
A program may use at most 128 MiB of HBM per device.

```python
import jax
import jax.numpy as jnp
from jax import lax

B = 128
M = 128
STEPS = 4
NBR = 9
NCX = 128
NCY = 64


def level_of(key, extent, shards, least, high):
    factor_of, own = 1.0, jax.random.fold_in(key, 6)
    for position, parts in shards:
        heights = jnp.exp(jax.random.uniform(jax.random.fold_in(own, position), (parts,), jnp.float32, least / len(shards), high / len(shards)))
        factor_of = factor_of * jnp.repeat(heights, extent[position] // parts).reshape([-1 if axis == position else 1 for axis in range(len(extent))])
    return factor_of


def noise(stream_key, extent, width, most, cuts=(), kind=jnp.bfloat16):
    drawn = width * jax.random.normal(stream_key, extent, jnp.float32)
    if cuts:
        drawn = drawn * level_of(stream_key, extent, cuts, -0.22, 0.18)
    return jnp.clip(drawn, -most, most).astype(kind)


def setup_inputs(seed: int = 0) -> dict:
    seeds = jax.random.split(jax.random.key(seed), 4)
    return {
        "vectors": noise(seeds[0], (NCX, NCY, B, M), 1.0, 6.0, ((0, 32), (1, 8))),
        "hamiltonian": noise(seeds[1], (NCX, NCY, NBR, B, B), (2 * NBR * B) ** -0.5, 0.125, ((0, 32), (1, 8))),
        "neighbours": jax.vmap(lambda own: jax.random.permutation(own, NBR))(jax.random.split(seeds[2], NCX * NCY)).reshape((NCX, NCY, NBR)).astype(jnp.int32),
    }


def operate(current_b, hamiltonian, neighbours):
    def one_row(row_index):
        nearby = [current_b[(row_index + offset_x) % NCX] for offset_x in (-1, 0, 1)]
        views = []
        for offset_x in (-1, 0, 1):
            for offset_y in (-1, 0, 1):
                views.append(jnp.roll(nearby[offset_x + 1], -offset_y, axis=0))
        stacked = jnp.stack(views, axis=1)
        chosen = jnp.take_along_axis(stacked, neighbours[row_index][:, :, None, None], axis=1)
        return jnp.einsum('ykij,ykjm->yim', hamiltonian[row_index].astype(jnp.float32), chosen.astype(jnp.float32))
    return lax.map(one_row, jnp.arange(NCX, dtype=jnp.int32))


def reference(vectors, hamiltonian, neighbours):
    previous = vectors.astype(jnp.float32)
    current = operate(vectors, hamiltonian, neighbours)
    for step_index in range(1, STEPS):
        following = 2.0 * operate(current.astype(jnp.bfloat16), hamiltonian, neighbours) - previous
        previous = current
        current = following
    return current
```

```python
import functools

import jax
import jax.numpy as jnp
from jax import lax
from jax.experimental import pallas as pl
from jax.experimental.pallas import tpu as pltpu
from jax.sharding import PartitionSpec as P

STEPS = 4
NBR = 9
VMEM = pl.BlockSpec(memory_space=pltpu.VMEM)
SMEM = pl.BlockSpec(memory_space=pltpu.SMEM)
LIMIT = 24 * 1024 * 1024


def product(blocks, fields):
    terms = [jnp.dot(h, v, preferred_element_type=jnp.float32) for h, v in zip(blocks, fields)]
    return functools.reduce(jnp.add, terms)


def local_kernel(first, rows, cols, *refs):
    if first:
        place, ham, field, total, rounded = refs
    else:
        place, ham, field, before, total, rounded = refs

    def cell(i, j, offsets_x, offsets_y, inside):
        codes = [(a, b) for a in offsets_x for b in offsets_y]
        blocks = [ham[i, j, place[(i * cols + j) * NBR + (a + 1) * 3 + b + 1]] for a, b in codes]
        value = product(blocks, [field[i + a, j + b] for a, b in codes])
        if not first:
            value = 2.0 * value - before[i, j].astype(jnp.float32)
        total[i, j] = value
        if inside:
            rounded[i, j] = value.astype(jnp.bfloat16)

    for i in range(rows):
        for j in range(cols):
            offsets_x = [a for a in (-1, 0, 1) if 0 <= i + a < rows]
            offsets_y = [b for b in (-1, 0, 1) if 0 <= j + b < cols]
            cell(i, j, offsets_x, offsets_y, len(offsets_x) * len(offsets_y) == NBR)


def rim_kernel(first, last, rows, cols, *refs):
    place, side, ham, near, far, even, odd, near2, far_even, far_odd, partial = refs[:11]
    if last:
        total, halo = refs[11:]
    else:
        total, rounded, *sends, halo = refs[12:]
    core, parity = side[0], side[1]
    row_near, row_far = (1 - core) * (rows + 1), core * (rows + 1)
    col_even, col_odd = (1 - parity) * (cols + 1), parity * (cols + 1)
    for j in range(cols):
        halo[row_near, j + 1] = near[j]
        halo[row_far, j + 1] = far[j]
    for i in range(rows):
        halo[i + 1, col_even] = even[i]
        halo[i + 1, col_odd] = odd[i]
    halo[row_near, col_even] = near2[0]
    halo[row_near, col_odd] = near2[1]
    halo[row_far, col_even] = far_even[...]
    halo[row_far, col_odd] = far_odd[...]

    for i in range(rows):
        for j in range(cols):
            codes = [
                (a, b)
                for a in (-1, 0, 1)
                for b in (-1, 0, 1)
                if not (0 <= i + a < rows and 0 <= j + b < cols)
            ]
            if codes:
                blocks = [ham[i, j, place[(i * cols + j) * NBR + (a + 1) * 3 + b + 1]] for a, b in codes]
                value = product(blocks, [halo[i + 1 + a, j + 1 + b] for a, b in codes])
                value = partial[i, j] + (value if first else 2.0 * value)
                total[i, j] = value
                if not last:
                    rounded[i, j] = value.astype(jnp.bfloat16)
            elif last:
                total[i, j] = partial[i, j]
    if not last:
        fill_edges(rounded, core, parity, rows, cols, *sends)


def fill_edges(field, core, parity, rows, cols, near, far, even, odd, far_even, far_odd):
    row_near, row_far = (1 - core) * (rows - 1), core * (rows - 1)
    col_even, col_odd = (1 - parity) * (cols - 1), parity * (cols - 1)
    for j in range(cols):
        near[j] = field[row_near, j]
        far[j] = field[row_far, j]
    for i in range(rows):
        even[i] = field[i, col_even]
        odd[i] = field[i, col_odd]
    far_even[...] = field[row_far, col_even]
    far_odd[...] = field[row_far, col_odd]


def edge_kernel(rows, cols, side, field, *sends):
    fill_edges(field, side[0], side[1], rows, cols, *sends)


def swaps(size_x, size_y):
    def pairs(move):
        out = []
        for x in range(size_x):
            for y in range(size_y):
                a, b = move(x, y)
                out.append((x * size_y + y, (a % size_x) * size_y + b % size_y))
        return out

    near = pairs(lambda x, y: (x ^ 1, y))
    far = pairs(lambda x, y: (x - 1 + 2 * (x % 2), y))
    even = pairs(lambda x, y: (x, y ^ 1))
    odd = pairs(lambda x, y: (x, y - 1 + 2 * (y % 2)))
    far_even = pairs(lambda x, y: (x - 1 + 2 * (x % 2), y ^ 1))
    far_odd = pairs(lambda x, y: (x - 1 + 2 * (x % 2), y - 1 + 2 * (y % 2)))
    return near, far, even, odd, far_even, far_odd


def on_device(vectors, hamiltonian, neighbours):
    rows, cols, size, trials = vectors.shape
    axes = ("gx", "gy")
    pairs = swaps(lax.axis_size("gx"), lax.axis_size("gy"))
    core = lax.axis_index("gx") % 2
    parity = lax.axis_index("gy") % 2
    side = jnp.stack([core, parity]).astype(jnp.int32)
    codes = jnp.arange(NBR, dtype=jnp.int32)
    hit = neighbours[:, :, None, :] == codes[:, None]
    place = jnp.sum(jnp.where(hit, codes, 0), axis=-1, dtype=jnp.int32).reshape(-1)

    def shape(*dims, dtype=jnp.bfloat16):
        return jax.ShapeDtypeStruct((*dims, size, trials), dtype)

    sends = (shape(cols), shape(cols), shape(rows), shape(rows), shape(), shape())
    params = pltpu.CompilerParams(vmem_limit_bytes=LIMIT)

    def cost(products):
        return pl.CostEstimate(flops=products * 2 * size * size * trials, bytes_accessed=products * 2 * size * size, transcendentals=0)

    edges = pl.pallas_call(
        functools.partial(edge_kernel, rows, cols),
        out_shape=sends,
        in_specs=[SMEM, VMEM],
        out_specs=[VMEM] * len(sends),
        compiler_params=params,
        name="edges",
    )(side, vectors)

    def travel(edges):
        near, far, even, odd, far_even, far_odd = [
            lax.ppermute(sent, axes, pair) for sent, pair in zip(edges, pairs)
        ]
        row_near = (1 - core) * (rows - 1)
        both = jnp.stack([lax.dynamic_index_in_dim(v, row_near, keepdims=False) for v in (even, odd)])
        near2 = lax.ppermute(both, axes, pairs[0])
        return near, far, even, odd, near2, far_even, far_odd

    field, before = vectors, None
    for step in range(STEPS):
        first, last = step == 0, step == STEPS - 1
        halos = travel(edges)
        extra = () if first else (before,)
        partial, rounded = pl.pallas_call(
            functools.partial(local_kernel, first, rows, cols),
            out_shape=(shape(rows, cols, dtype=jnp.float32), shape(rows, cols)),
            in_specs=[SMEM] + [VMEM] * (2 + len(extra)),
            out_specs=[VMEM] * 2,
            compiler_params=params,
            cost_estimate=cost(220),
            name="local",
        )(place, hamiltonian, field, *extra)
        common = (place, side, hamiltonian, *halos, partial)
        scratch = [pltpu.VMEM((rows + 2, cols + 2, size, trials), jnp.bfloat16)]
        if last:
            return pl.pallas_call(
                functools.partial(rim_kernel, first, last, rows, cols),
                out_shape=shape(rows, cols, dtype=jnp.float32),
                in_specs=[SMEM] * 2 + [VMEM] * 9,
                out_specs=VMEM,
                scratch_shapes=scratch,
                compiler_params=params,
                cost_estimate=cost(68),
                name="rim",
            )(*common)
        total, rounded, *edges = pl.pallas_call(
            functools.partial(rim_kernel, first, last, rows, cols),
            out_shape=(shape(rows, cols, dtype=jnp.float32), shape(rows, cols), *sends),
            in_specs=[SMEM] * 2 + [VMEM] * 10,
            out_specs=[VMEM] * 8,
            scratch_shapes=scratch,
            input_output_aliases={10: 0, 11: 1},
            compiler_params=params,
            cost_estimate=cost(68),
            name="rim",
        )(*common, rounded)
        before, field = (field if first else before_next), rounded
        before_next = total


def solution(mesh):
    placed = (P("gx", "gy", None, None), P("gx", "gy", None, None, None), P("gx", "gy", None))
    return jax.shard_map(
        on_device, mesh=mesh, in_specs=placed, out_specs=P("gx", "gy", None, None), check_vma=False
    )
```

```python
import functools

import jax
import jax.numpy as jnp
from jax import lax
from jax.experimental import pallas as pl
from jax.experimental.pallas import tpu as pltpu
from jax.sharding import PartitionSpec as P

STEPS = 4
NBR = 9
VMEM = pl.BlockSpec(memory_space=pltpu.VMEM)
SMEM = pl.BlockSpec(memory_space=pltpu.SMEM)
HBM = pl.BlockSpec(memory_space=pltpu.HBM)
LIMIT = 16 * 1024 * 1024


def product(terms):
    return functools.reduce(
        jnp.add, [jnp.dot(h, v, preferred_element_type=jnp.float32) for h, v in terms]
    )


def edge_kernel(rows, cols, side, field, near, far, even, odd, far_even, far_odd):
    core, parity = side[0], side[1]
    row_near, row_far = (1 - core) * (rows - 1), core * (rows - 1)
    col_even, col_odd = (1 - parity) * (cols - 1), parity * (cols - 1)
    for i in range(rows):
        even[i] = field[i, col_even]
        odd[i] = field[i, col_odd]
    for j in range(cols):
        near[j] = field[row_near, j]
        far[j] = field[row_far, j]
    far_even[...] = field[row_far, col_even]
    far_odd[...] = field[row_far, col_odd]


def lines(side, rows, cols):
    core, parity = side[0], side[1]
    lines_x = (((1 - core) * (rows - 1), 1 - 2 * core), (core * (rows - 1), 2 * core - 1))
    lines_y = (((1 - parity) * (cols - 1), 1 - 2 * parity), (parity * (cols - 1), 2 * parity - 1))
    return lines_x, lines_y


def rim_codes(side, rows, cols):
    lines_x, lines_y = lines(side, rows, cols)
    for j, b in lines_y:
        for i, a in lines_x:
            yield i, j, ((a, 0), (a, -b), (0, b), (-a, b), (a, b))
        for i in range(1, rows - 1):
            yield i, j, [(c, b) for c in (-1, 0, 1)]
    for i, a in lines_x:
        for j in range(1, cols - 1):
            yield i, j, [(a, c) for c in (-1, 0, 1)]


def first_kernel(rows, cols, listed, stored, field, ham, place, total, rounded, sems):
    copies = [pltpu.make_async_copy(stored.at[i], ham.at[i], sems.at[i]) for i in range(rows)]
    for copy in copies:
        copy.start()
    for i in range(rows):
        for j in range(cols):
            for k in range(NBR):
                place[(i * cols + j) * NBR + listed[i, j, k]] = k
    for i in range(rows):
        copies[i].wait()
        local_row(i, rows, cols, place, ham, field, None, total, rounded)


def local_kernel(chosen, rows, cols, outs, place, ham, field, before, *refs):
    total, rounded = (*refs[-outs:], None)[:2]
    for i in chosen:
        local_row(i, rows, cols, place, ham, field, before, total, rounded)


def local_row(i, rows, cols, place, ham, field, before, total, rounded):
    for j in range(cols):
        codes = [
            (a, b)
            for a in (-1, 0, 1)
            for b in (-1, 0, 1)
            if 0 <= i + a < rows and 0 <= j + b < cols
        ]
        value = product(
            [
                (ham[i, j, place[(i * cols + j) * NBR + (a + 1) * 3 + b + 1]], field[i + a, j + b])
                for a, b in codes
            ]
        )
        if before is not None:
            value = 2.0 * value - before[i, j].astype(jnp.float32)
        total[i, j] = value
        if len(codes) == NBR and rounded is not None:
            rounded[i, j] = value.astype(jnp.bfloat16)


def rim_kernel(first, last, rows, cols, place, side, ham, far, even, odd, near2, far_even, far_odd, near, partial, *refs):
    if last:
        total, stored, sems = refs
    else:
        total, rounded, send_near, send_far, send_even, send_odd, send_far_even, send_far_odd = refs[1:]
    lines_x, lines_y = lines(side, rows, cols)
    halos_x, halos_y = (near, far), (even, odd)
    corners = ((near2.at[0], near2.at[1]), (far_even, far_odd))
    cells = rim_codes(side, rows, cols)
    copies = []

    def store(*place):
        if last:
            copies.append(pltpu.make_async_copy(total.at[place], stored.at[place], sems.at[len(copies)]))
            copies[-1].start()

    def cell(fields):
        i, j, codes = next(cells)
        base = (i * cols + j) * NBR + 4
        blocks = [ham[i, j, place[base + a * 3 + b]] for a, b in codes]
        value = product(list(zip(blocks, fields)))
        value = partial[i, j] + (value if first else 2.0 * value)
        total[i, j] = value
        if last:
            return None
        value = value.astype(jnp.bfloat16)
        rounded[i, j] = value
        return value

    for i in range(1, rows - 1):
        store(i, pl.ds(1, cols - 2))
    for y, (j, b) in enumerate(lines_y):
        halo_y = halos_y[y]
        for x, (i, a) in enumerate(lines_x):
            halo_x = halos_x[x]
            value = cell((halo_x[j], halo_x[j - b], halo_y[i], halo_y[i - a], corners[x][y][...]))
            if not last:
                (send_near, send_far)[x][j] = value
                (send_even, send_odd)[y][i] = value
                if x == 1:
                    (send_far_even, send_far_odd)[y][...] = value
        for i in range(1, rows - 1):
            value = cell([halo_y[i + c] for c in (-1, 0, 1)])
            if not last:
                (send_even, send_odd)[y][i] = value
        store(pl.ds(1, rows - 2), j)
    for x, (i, a) in enumerate(lines_x):
        for j in range(1, cols - 1):
            value = cell([halos_x[x][j + c] for c in (-1, 0, 1)])
            if not last:
                (send_near, send_far)[x][j] = value
        store(i)
    for copy in copies:
        copy.wait()


def swaps(size_x, size_y):
    def pairs(move):
        out = []
        for x in range(size_x):
            for y in range(size_y):
                a, b = move(x, y)
                out.append((x * size_y + y, (a % size_x) * size_y + b % size_y))
        return out

    def far(x):
        return x - 1 + 2 * (x % 2)

    def odd(y):
        return y - 1 + 2 * (y % 2)

    return dict(
        near=pairs(lambda x, y: (x ^ 1, y)),
        far=pairs(lambda x, y: (far(x), y)),
        even=pairs(lambda x, y: (x, y ^ 1)),
        odd=pairs(lambda x, y: (x, odd(y))),
        far_even=pairs(lambda x, y: (far(x), y ^ 1)),
        far_odd=pairs(lambda x, y: (far(x), odd(y))),
    )


def on_device(vectors, hamiltonian, neighbours):
    rows, cols, size, trials = vectors.shape
    axes = ("gx", "gy")
    pairs = swaps(lax.axis_size("gx"), lax.axis_size("gy"))
    core = lax.axis_index("gx") % 2
    parity = lax.axis_index("gy") % 2
    side = jnp.stack([core, parity]).astype(jnp.int32)

    def shape(*dims, dtype=jnp.bfloat16):
        return jax.ShapeDtypeStruct((*dims, size, trials), dtype)

    sends = (shape(cols), shape(cols), shape(rows), shape(rows), shape(), shape())
    params = pltpu.CompilerParams(vmem_limit_bytes=LIMIT)

    def cost(products):
        return pl.CostEstimate(
            flops=products * 2 * size * size * trials,
            bytes_accessed=products * 2 * size * size,
            transcendentals=0,
        )

    edges = pl.pallas_call(
        functools.partial(edge_kernel, rows, cols),
        out_shape=sends,
        in_specs=[SMEM, VMEM],
        out_specs=[VMEM] * len(sends),
        compiler_params=params,
        name="edges",
    )(side, vectors)

    def depart(edges):
        names = ("near", "far", "even", "odd", "far_even", "far_odd")
        return [lax.ppermute(sent, axes, pairs[name]) for sent, name in zip(edges, names)]

    def pass_on(even, odd):
        row_near = (1 - core) * (rows - 1)
        both = jnp.stack([lax.dynamic_index_in_dim(v, row_near, keepdims=False) for v in (even, odd)])
        return lax.ppermute(both, axes, pairs["near"])

    def local(kept, chosen, *operands):
        done = len(operands) - 4
        return pl.pallas_call(
            functools.partial(local_kernel, chosen, rows, cols, len(kept)),
            out_shape=kept,
            in_specs=[SMEM] + [VMEM] * (len(operands) - 1),
            out_specs=[VMEM] * len(kept),
            input_output_aliases={4 + i: i for i in range(done)},
            compiler_params=params,
            cost_estimate=cost(55 * len(chosen)),
            name="local",
        )(*operands)

    field, before, newest = vectors, None, None
    for step in range(STEPS):
        first, last = step == 0, step == STEPS - 1
        near, far, even, odd, far_even, far_odd = depart(edges)
        both = (shape(rows, cols, dtype=jnp.float32), shape(rows, cols))
        kept = both[:1] if last else both
        if first:
            hamiltonian, place, partial, *rounded = pl.pallas_call(
                functools.partial(first_kernel, rows, cols),
                out_shape=(
                    jax.ShapeDtypeStruct(hamiltonian.shape, hamiltonian.dtype),
                    jax.ShapeDtypeStruct((neighbours.size,), jnp.int32),
                    *kept,
                ),
                in_specs=[SMEM, HBM, VMEM],
                out_specs=[VMEM, SMEM, VMEM, VMEM],
                scratch_shapes=[pltpu.SemaphoreType.DMA((rows,))],
                compiler_params=params,
                cost_estimate=cost(220),
                name="local",
            )(neighbours, pltpu.with_memory_space_constraint(hamiltonian, pltpu.HBM), field)
            near2 = pass_on(even, odd)
        else:
            fixed = (place, hamiltonian, field, before)
            begun = local(kept, range(rows), *fixed)
            even, odd, far_even, far_odd, begun = lax.optimization_barrier(
                (even, odd, far_even, far_odd, tuple(begun))
            )
            near2 = pass_on(even, odd)
            partial, *rounded = begun
        operands = (place, side, hamiltonian)
        operands += (far, even, odd, near2, far_even, far_odd, near, partial, *rounded)
        out = pl.pallas_call(
            functools.partial(rim_kernel, first, last, rows, cols),
            out_shape=kept + (kept if last else sends),
            in_specs=[SMEM] * 2 + [VMEM] * (len(operands) - 2),
            out_specs=[VMEM, HBM] if last else [VMEM] * (2 + len(sends)),
            scratch_shapes=[pltpu.SemaphoreType.DMA((rows + 2,))] if last else [],
            input_output_aliases={10: 0} if last else {10: 0, 11: 1},
            compiler_params=params,
            cost_estimate=cost(68),
            name="rim",
        )(*operands)
        if last:
            return out[1]
        total, rounded, *edges = out
        before, newest = vectors if first else newest, total
        field = rounded


def solution(mesh):
    placed = (P("gx", "gy", None, None), P("gx", "gy", None, None, None), P("gx", "gy", None))
    return jax.shard_map(
        on_device, mesh=mesh, in_specs=placed, out_specs=P("gx", "gy", None, None), check_vma=False
    )
```

```python
import functools

import jax
import jax.numpy as jnp
from jax import lax
from jax.experimental import pallas as pl
from jax.experimental.pallas import tpu as pltpu
from jax.sharding import PartitionSpec as P

STEPS = 4
NBR = 9
VMEM = pl.BlockSpec(memory_space=pltpu.VMEM)
SMEM = pl.BlockSpec(memory_space=pltpu.SMEM)
HBM = pl.BlockSpec(memory_space=pltpu.HBM)
LIMIT = 16 * 1024 * 1024


def product(terms):
    return functools.reduce(
        jnp.add, [jnp.dot(h, v, preferred_element_type=jnp.float32) for h, v in terms]
    )


def edge_kernel(rows, cols, side, field, near, far, even, odd, far_even, far_odd):
    core, parity = side[0], side[1]
    row_near, row_far = (1 - core) * (rows - 1), core * (rows - 1)
    col_even, col_odd = (1 - parity) * (cols - 1), parity * (cols - 1)
    for i in range(rows):
        even[i] = field[i, col_even]
        odd[i] = field[i, col_odd]
    for j in range(cols):
        near[j] = field[row_near, j]
        far[j] = field[row_far, j]
    far_even[...] = field[row_far, col_even]
    far_odd[...] = field[row_far, col_odd]


def lines(side, rows, cols):
    core, parity = side[0], side[1]
    lines_x = (((1 - core) * (rows - 1), 1 - 2 * core), (core * (rows - 1), 2 * core - 1))
    lines_y = (((1 - parity) * (cols - 1), 1 - 2 * parity), (parity * (cols - 1), 2 * parity - 1))
    return lines_x, lines_y


def rim_codes(side, rows, cols):
    lines_x, lines_y = lines(side, rows, cols)
    for j, b in lines_y:
        for i, a in lines_x:
            yield i, j, ((a, 0), (a, -b), (0, b), (-a, b), (a, b))
        for i in range(1, rows - 1):
            yield i, j, [(c, b) for c in (-1, 0, 1)]
    for i, a in lines_x:
        for j in range(1, cols - 1):
            yield i, j, [(a, c) for c in (-1, 0, 1)]


def first_kernel(rows, cols, listed, stored, vectors, ham, place, total, rounded, field, sems):
    fetch = pltpu.make_async_copy(vectors, field, sems.at[rows])
    fetch.start()
    copies = [pltpu.make_async_copy(stored.at[i], ham.at[i], sems.at[i]) for i in range(rows)]
    for copy in copies:
        copy.start()
    for i in range(rows):
        for j in range(cols):
            for k in range(NBR):
                place[(i * cols + j) * NBR + listed[i, j, k]] = k
    fetch.wait()
    for i in range(rows):
        copies[i].wait()
        local_row(i, rows, cols, place, ham, field, None, total, rounded)


def local_kernel(chosen, rows, cols, outs, place, ham, field, before, *refs):
    total, rounded = (*refs[-outs:], None)[:2]
    for i in chosen:
        local_row(i, rows, cols, place, ham, field, before, total, rounded)


def local_row(i, rows, cols, place, ham, field, before, total, rounded):
    for j in range(cols):
        codes = [
            (a, b)
            for a in (-1, 0, 1)
            for b in (-1, 0, 1)
            if 0 <= i + a < rows and 0 <= j + b < cols
        ]
        value = product(
            [
                (ham[i, j, place[(i * cols + j) * NBR + (a + 1) * 3 + b + 1]], field[i + a, j + b])
                for a, b in codes
            ]
        )
        if before is not None:
            value = 2.0 * value - before[i, j].astype(jnp.float32)
        total[i, j] = value
        if len(codes) == NBR and rounded is not None:
            rounded[i, j] = value.astype(jnp.bfloat16)


def rim_kernel(first, last, rows, cols, place, side, ham, far, even, odd, near2, far_even, far_odd, near, partial, *refs):
    if last:
        total, stored, sems = refs
    else:
        total, rounded, send_near, send_far, send_even, send_odd, send_far_even, send_far_odd = refs[1:]
    lines_x, lines_y = lines(side, rows, cols)
    halos_x, halos_y = (near, far), (even, odd)
    corners = ((near2.at[0], near2.at[1]), (far_even, far_odd))
    cells = rim_codes(side, rows, cols)
    copies = []

    def store(*place):
        if last:
            copies.append(pltpu.make_async_copy(total.at[place], stored.at[place], sems.at[len(copies)]))
            copies[-1].start()

    def cell(fields):
        i, j, codes = next(cells)
        base = (i * cols + j) * NBR + 4
        blocks = [ham[i, j, place[base + a * 3 + b]] for a, b in codes]
        value = product(list(zip(blocks, fields)))
        value = partial[i, j] + (value if first else 2.0 * value)
        total[i, j] = value
        if last:
            return None
        value = value.astype(jnp.bfloat16)
        rounded[i, j] = value
        return value

    for i in range(1, rows - 1):
        store(i, pl.ds(1, cols - 2))
    for y, (j, b) in enumerate(lines_y):
        halo_y = halos_y[y]
        for x, (i, a) in enumerate(lines_x):
            halo_x = halos_x[x]
            value = cell((halo_x[j], halo_x[j - b], halo_y[i], halo_y[i - a], corners[x][y][...]))
            if not last:
                (send_near, send_far)[x][j] = value
                (send_even, send_odd)[y][i] = value
                if x == 1:
                    (send_far_even, send_far_odd)[y][...] = value
        for i in range(1, rows - 1):
            value = cell([halo_y[i + c] for c in (-1, 0, 1)])
            if not last:
                (send_even, send_odd)[y][i] = value
        store(pl.ds(1, rows - 2), j)
    for x, (i, a) in enumerate(lines_x):
        for j in range(1, cols - 1):
            value = cell([halos_x[x][j + c] for c in (-1, 0, 1)])
            if not last:
                (send_near, send_far)[x][j] = value
        store(i)
    for copy in copies:
        copy.wait()


def swaps(size_x, size_y):
    def pairs(move):
        out = []
        for x in range(size_x):
            for y in range(size_y):
                a, b = move(x, y)
                out.append((x * size_y + y, (a % size_x) * size_y + b % size_y))
        return out

    def far(x):
        return x - 1 + 2 * (x % 2)

    def odd(y):
        return y - 1 + 2 * (y % 2)

    return dict(
        near=pairs(lambda x, y: (x ^ 1, y)),
        far=pairs(lambda x, y: (far(x), y)),
        even=pairs(lambda x, y: (x, y ^ 1)),
        odd=pairs(lambda x, y: (x, odd(y))),
        far_even=pairs(lambda x, y: (far(x), y ^ 1)),
        far_odd=pairs(lambda x, y: (far(x), odd(y))),
    )


def on_device(vectors, hamiltonian, neighbours):
    rows, cols, size, trials = vectors.shape
    axes = ("gx", "gy")
    pairs = swaps(lax.axis_size("gx"), lax.axis_size("gy"))
    core = lax.axis_index("gx") % 2
    parity = lax.axis_index("gy") % 2
    side = jnp.stack([core, parity]).astype(jnp.int32)

    def shape(*dims, dtype=jnp.bfloat16):
        return jax.ShapeDtypeStruct((*dims, size, trials), dtype)

    sends = (shape(cols), shape(cols), shape(rows), shape(rows), shape(), shape())
    params = pltpu.CompilerParams(vmem_limit_bytes=LIMIT)

    def cost(products):
        return pl.CostEstimate(
            flops=products * 2 * size * size * trials,
            bytes_accessed=products * 2 * size * size,
            transcendentals=0,
        )

    edges = pl.pallas_call(
        functools.partial(edge_kernel, rows, cols),
        out_shape=sends,
        in_specs=[SMEM, VMEM],
        out_specs=[VMEM] * len(sends),
        compiler_params=params,
        name="edges",
    )(side, vectors)

    def depart(edges):
        names = ("near", "far", "even", "odd", "far_even", "far_odd")
        return [lax.ppermute(sent, axes, pairs[name]) for sent, name in zip(edges, names)]

    def pass_on(even, odd):
        row_near = (1 - core) * (rows - 1)
        both = jnp.stack([lax.dynamic_index_in_dim(v, row_near, keepdims=False) for v in (even, odd)])
        return lax.ppermute(both, axes, pairs["near"])

    def local(kept, chosen, *operands):
        done = len(operands) - 4
        return pl.pallas_call(
            functools.partial(local_kernel, chosen, rows, cols, len(kept)),
            out_shape=kept,
            in_specs=[SMEM] + [VMEM] * (len(operands) - 1),
            out_specs=[VMEM] * len(kept),
            input_output_aliases={4 + i: i for i in range(done)},
            compiler_params=params,
            cost_estimate=cost(55 * len(chosen)),
            name="local",
        )(*operands)

    field, before, newest = vectors, None, None
    for step in range(STEPS):
        first, last = step == 0, step == STEPS - 1
        near, far, even, odd, far_even, far_odd = depart(edges)
        both = (shape(rows, cols, dtype=jnp.float32), shape(rows, cols))
        kept = both[:1] if last else both
        if first:
            hamiltonian, place, partial, *rounded = pl.pallas_call(
                functools.partial(first_kernel, rows, cols),
                out_shape=(
                    jax.ShapeDtypeStruct(hamiltonian.shape, hamiltonian.dtype),
                    jax.ShapeDtypeStruct((neighbours.size,), jnp.int32),
                    *kept,
                ),
                in_specs=[SMEM, HBM, HBM],
                out_specs=[VMEM, SMEM, VMEM, VMEM],
                scratch_shapes=[
                    pltpu.VMEM(field.shape, field.dtype),
                    pltpu.SemaphoreType.DMA((rows + 1,)),
                ],
                compiler_params=params,
                cost_estimate=cost(220),
                name="local",
            )(
                neighbours,
                pltpu.with_memory_space_constraint(hamiltonian, pltpu.HBM),
                pltpu.with_memory_space_constraint(field, pltpu.HBM),
            )
            near2 = pass_on(even, odd)
        else:
            fixed = (place, hamiltonian, field, before)
            begun = local(kept, range(0, rows - 1), *fixed)
            even, odd, far_even, far_odd, begun = lax.optimization_barrier(
                (even, odd, far_even, far_odd, tuple(begun))
            )
            near2 = pass_on(even, odd)
            partial, *rounded = local(kept, range(rows - 1, rows), *fixed, *begun)
        operands = (place, side, hamiltonian)
        operands += (far, even, odd, near2, far_even, far_odd, near, partial, *rounded)
        out = pl.pallas_call(
            functools.partial(rim_kernel, first, last, rows, cols),
            out_shape=kept + (kept if last else sends),
            in_specs=[SMEM] * 2 + [VMEM] * (len(operands) - 2),
            out_specs=[VMEM, HBM] if last else [VMEM] * (2 + len(sends)),
            scratch_shapes=[pltpu.SemaphoreType.DMA((rows + 2,))] if last else [],
            input_output_aliases={10: 0} if last else {10: 0, 11: 1},
            compiler_params=params,
            cost_estimate=cost(68),
            name="rim",
        )(*operands)
        if last:
            return out[1]
        total, rounded, *edges = out
        before, newest = vectors if first else newest, total
        field = rounded


def solution(mesh):
    placed = (P("gx", "gy", None, None), P("gx", "gy", None, None, None), P("gx", "gy", None))
    return jax.shard_map(
        on_device, mesh=mesh, in_specs=placed, out_specs=P("gx", "gy", None, None), check_vma=False
    )
```
